32 devices in a mesh: groups: 2 (over y), tm: 4 (over z), segment: 2 (over x), head: 2 (over core).
Axes of the slice: x: 2, y: 2, z: 4, core: 2. Of those that a mesh axis runs over, the one named last changes fastest.
Arguments:
- hidden_in: bfloat16 [768, 3072], P(('groups', 'tm'), 'head'), parts along dimension 0, may hold values from -6 to 6
- key_cache: bfloat16 [2, 768, 3072], P('segment', ('groups', 'tm'), 'head'), parts along dimension 1, may hold values from -6 to 6
- value_cache: bfloat16 [2, 768, 3072], P('segment', ('groups', 'tm'), 'head'), parts along dimension 1, may hold values from -6 to 6
- query_gain: float32 [2, 128], P('segment'), may hold values from 0.4 to 1.6
- key_gain: float32 [2, 128], P('segment'), may hold values from 0.4 to 1.6
- out_gate: float32 [2, 3072], P('segment', 'head'), may hold values from 0.5 to 2
- span_ids: int32 [768], P('groups'), parts along dimension 0, may hold values from 0 to 2, as said below
Outputs:
- layer_outputs: bfloat16 [2, 768, 3072], P('segment', ('groups', 'tm'), 'head'), parts along dimension 1
The draws below stay inside these ranges and needn't reach their ends.
There are 2 independent parts, one for each index of `groups`. The reference program is written for one: setup_inputs(seed, part) draws one part's arguments, and reference() takes and returns one part's arrays. A program takes and returns all parts, laid end to end along the dimension named above; an argument that names none is the same for every part. Nothing has to cross between parts.
Inputs may be any that keep to these rules, and one draw needn't show every extreme that they name: span_ids never fall and rise by one from span to span; every span but the first and the last holds exactly 192 tokens, and the first and the last together hold 192, each at least one.
All inputs are finite; a program needn't handle non-finite values.
Results may differ from the reference program's by a relative error of at most 0.011.
Values may be sent and summed in bfloat16 or wider, within the bound.
No kernel may reach another device: no remote copies, remote signals or barrier semaphores. Data moves between devices by JAX's collectives and lax.ppermute only.
A program may use at most 64 MiB of HBM per device.

```python
import math
import jax
import jax.numpy as jnp
from jax import lax

HEAD_DIM = 128
TOK_DEV = 96
TOKENS = 384
LAYERS = 2
FEATURES = 3072
N_TM = 4


def draw_span_ids(key, part):
    inside = jax.random.randint(jax.random.fold_in(key, 11), (), 1, TOK_DEV)
    upper_half = jax.random.randint(jax.random.fold_in(key, 12), (), 0, 2)
    offset = inside + upper_half * TOK_DEV
    positions = jnp.arange(TOKENS, dtype=jnp.int32)
    return ((positions + offset) // (2 * TOK_DEV)).astype(jnp.int32)


def level_of(key, extent, pieces, smallest, largest):
    gain, own = 1.0, jax.random.fold_in(key, 6)
    for axis_at, parts in pieces:
        draws = jnp.exp(jax.random.uniform(jax.random.fold_in(own, axis_at), (parts,), jnp.float32, smallest / len(pieces), largest / len(pieces)))
        gain = gain * jnp.repeat(draws, extent[axis_at] // parts).reshape([-1 if axis == axis_at else 1 for axis in range(len(extent))])
    return gain


def gaussian(own_key, extent, scale, reach, shards=(), kind=jnp.bfloat16):
    entries = jax.random.normal(own_key, extent, jnp.float32) * scale
    if len(shards) > 0:
        entries = level_of(own_key, extent, shards, -0.22, 0.18) * entries
    return jnp.clip(entries, min=-reach, max=reach).astype(kind)


def setup_inputs(seed: int = 0, part: int = 0) -> dict:
    arg_keys = jax.random.split(jax.random.key(seed), 8)
    own_keys = jax.random.split(jax.random.fold_in(arg_keys[7], part), 8)
    return {
        "hidden_in": gaussian(own_keys[0], (TOKENS, FEATURES), 1.0, 6.0, ((0, 4), (1, 2))),
        "key_cache": gaussian(own_keys[1], (LAYERS, TOKENS, FEATURES), 1.0, 6.0, ((0, 2), (1, 4), (2, 2))),
        "value_cache": gaussian(own_keys[2], (LAYERS, TOKENS, FEATURES), 1.0, 6.0, ((0, 2), (1, 4), (2, 2))),
        "query_gain": jnp.clip(1.0 + 0.12 * jax.random.normal(arg_keys[3], (LAYERS, HEAD_DIM), jnp.float32), 0.4, 1.6),
        "key_gain": jnp.clip(1.0 + 0.12 * jax.random.normal(arg_keys[4], (LAYERS, HEAD_DIM), jnp.float32), 0.4, 1.6),
        "out_gate": jnp.clip(0.5 + 1.5 * jax.random.uniform(arg_keys[5], (LAYERS, FEATURES), jnp.float32) ** level_of(arg_keys[5], (LAYERS, FEATURES), ((0, 2), (1, 2)), -0.2, 0.2), 0.5, 2.0),
        "span_ids": draw_span_ids(jax.random.fold_in(jax.random.fold_in(arg_keys[7], part), 71), part),
    }


def head_normalize(features, gain_row):
    row_count = features.shape[0]
    shaped = features.astype(jnp.float32).reshape(row_count, -1, HEAD_DIM)
    inverse_rms = lax.rsqrt(lax.optimization_barrier(jnp.mean(shaped * shaped, axis=-1, keepdims=True)) + 1e-06)
    return (shaped * inverse_rms * gain_row).reshape(features.shape).astype(jnp.bfloat16)

def attend_block(queries, key_rows, value_rows, query_ids, key_ids):
    row_count = queries.shape[0]
    head_count = queries.shape[1] // HEAD_DIM
    score_scale = 2.0 / math.sqrt(HEAD_DIM)
    query_heads = queries.astype(jnp.float32).reshape(row_count, head_count, HEAD_DIM)
    key_heads = key_rows.astype(jnp.float32).reshape(key_rows.shape[0], head_count, HEAD_DIM)
    value_heads = value_rows.astype(jnp.float32).reshape(value_rows.shape[0], head_count, HEAD_DIM)
    scores = jnp.einsum('rhd,khd->hrk', query_heads, key_heads) * score_scale
    allowed = (key_ids[None, :] <= query_ids[:, None]) & (key_ids[None, :] >= query_ids[:, None] - 2)
    weights = jnp.where(allowed[None], jnp.exp(scores), 0.0)
    denominator = lax.optimization_barrier(jnp.sum(weights, axis=-1))
    rounded = weights.astype(jnp.bfloat16).astype(jnp.float32)
    mixture = jnp.einsum('hrk,khd->rhd', rounded, value_heads)
    mixture = mixture / jnp.transpose(denominator)[:, :, None]
    return mixture.reshape(row_count, head_count * HEAD_DIM)

def reference(hidden_in, key_cache, value_cache, query_gain, key_gain, out_gate, span_ids):
    block_rows = TOK_DEV
    pad_back = 6 * block_rows
    pad_ahead = 2 * block_rows
    window_rows = 9 * block_rows
    filler_back = jnp.full((pad_back,), -1000, jnp.int32)
    filler_ahead = jnp.full((pad_ahead,), -1000, jnp.int32)
    padded_ids = jnp.concatenate([filler_back, span_ids.astype(jnp.int32), filler_ahead])
    current = hidden_in
    outputs = []
    for layer_index in range(LAYERS):
        normed_keys = head_normalize(key_cache[layer_index], key_gain[layer_index])
        padded_keys = jnp.pad(normed_keys, ((pad_back, pad_ahead), (0, 0)))
        padded_values = jnp.pad(value_cache[layer_index], ((pad_back, pad_ahead), (0, 0)))
        queries = head_normalize(current, query_gain[layer_index])

        def one_block(block_index):
            row_start = (block_index * block_rows).astype(jnp.int32)
            query_rows = lax.dynamic_slice_in_dim(queries, row_start, block_rows, 0)
            key_rows = lax.dynamic_slice_in_dim(padded_keys, row_start, window_rows, 0)
            value_rows = lax.dynamic_slice_in_dim(padded_values, row_start, window_rows, 0)
            query_ids = lax.dynamic_slice_in_dim(span_ids.astype(jnp.int32), row_start, block_rows, 0)
            key_ids = lax.dynamic_slice_in_dim(padded_ids, row_start, window_rows, 0)
            return attend_block(query_rows, key_rows, value_rows, query_ids, key_ids)
        mixture = lax.map(one_block, jnp.arange(N_TM, dtype=jnp.int32)).reshape(TOKENS, FEATURES)
        current = (current.astype(jnp.float32) + out_gate[layer_index] * mixture).astype(jnp.bfloat16)
        outputs.append(current)
    return jnp.stack(outputs)
```

```python
import functools
import math

import jax
import jax.numpy as jnp
from jax import lax
from jax.experimental import pallas as pl
from jax.experimental.pallas import tpu as pltpu
from jax.sharding import PartitionSpec as P

HEAD_DIM = 128
PART_ROWS = 16
BLOCKED = -1e30


def passed_along(shard, axis, by):
    devices = lax.axis_size(axis)
    pairs = [(i, i + by) for i in range(devices) if 0 <= i + by < devices]
    return lax.ppermute(shard, axis, pairs)


def head_normalize(features, gain_row):
    row_count = features.shape[0]
    shaped = features.astype(jnp.float32).reshape(row_count, -1, HEAD_DIM)
    inverse_rms = lax.rsqrt(jnp.mean(shaped * shaped, axis=-1, keepdims=True) + 1e-06)
    return (shaped * inverse_rms * gain_row).reshape(features.shape).astype(jnp.bfloat16)


def attend_heads(queries, key_rows, value_rows, query_ids, key_ids):
    row_count = queries.shape[0]
    key_count = key_rows.shape[0]
    pair_width = 2 * HEAD_DIM
    group_count = queries.shape[1] // pair_width
    score_scale = 2.0 / math.sqrt(HEAD_DIM)
    allowed = (key_ids[None, :] <= query_ids[:, None]) & (
        key_ids[None, :] >= query_ids[:, None] - 2
    )

    def pair_step(group_index, result):
        column = group_index * pair_width
        query_pair = lax.dynamic_slice_in_dim(queries, column, pair_width, 1).reshape(
            row_count, 2, HEAD_DIM
        )
        key_pair = lax.dynamic_slice_in_dim(key_rows, column, pair_width, 1).reshape(
            key_count, 2, HEAD_DIM
        )
        value_pair = lax.dynamic_slice_in_dim(value_rows, column, pair_width, 1).reshape(
            key_count, 2, HEAD_DIM
        )
        scores = (
            jnp.einsum("rhd,khd->hrk", query_pair, key_pair, preferred_element_type=jnp.float32)
            * score_scale
        )
        weights = jnp.where(allowed[None], jnp.exp(scores), 0.0)
        denominator = jnp.sum(weights, axis=-1)
        mixture = jnp.einsum(
            "hrk,khd->rhd",
            weights.astype(jnp.bfloat16),
            value_pair,
            preferred_element_type=jnp.float32,
        )
        mixture = mixture / jnp.transpose(denominator)[:, :, None]
        return lax.dynamic_update_slice_in_dim(
            result, mixture.reshape(row_count, pair_width), column, 1
        )

    initial = jnp.zeros((row_count, queries.shape[1]), jnp.float32)
    return lax.fori_loop(0, group_count, pair_step, initial)


def body(hidden_in, key_cache, value_cache, query_gain, key_gain, out_gate, span_ids):
    block_rows = hidden_in.shape[0]
    tm_index = lax.axis_index("tm")
    segment_index = lax.axis_index("segment")
    normed_keys = head_normalize(key_cache[0], key_gain[0])
    own_values = value_cache[0]
    first_row = tm_index * block_rows
    all_keys, all_values = (
        lax.all_gather(normed_keys, "tm", axis=0, tiled=True),
        lax.all_gather(own_values, "tm", axis=0, tiled=True),
    )

    def update(row_block):
        queries = head_normalize(row_block, query_gain[0])
        query_ids = lax.dynamic_slice_in_dim(span_ids, first_row, row_block.shape[0], 0)
        mixture = attend_heads(queries, all_keys, all_values, query_ids, span_ids)
        return (row_block.astype(jnp.float32) + out_gate[0] * mixture).astype(jnp.bfloat16)

    segments = lax.axis_size("segment")
    current = hidden_in
    result = hidden_in
    for section in range(segments):
        active = segment_index == section
        produced = lax.cond(active, lambda inputs: update(inputs), lambda inputs: inputs, current)
        result = jnp.where(active, produced, result)
        if section + 1 < segments:
            arrived = passed_along(produced, "segment", 1)
            current = jnp.where(segment_index == section + 1, arrived, current)
    return result[None]


MESH_TAIL = ("tm", "segment", "head")


def swapped(array, offset, blocks):
    at = lambda t, s, c: (t * 2 + s) * 2 + c
    pairs = [
        (at(t, s, c), at(t ^ offset, c, s))
        for t in range(blocks)
        for s in range(2)
        for c in range(2)
    ]
    return lax.ppermute(array, MESH_TAIL, pairs)


def normed(rows, gain):
    rows = rows.astype(jnp.float32)
    inverse_rms = lax.rsqrt(jnp.mean(rows * rows, axis=-1, keepdims=True) + 1e-06)
    return (rows * inverse_rms * gain).astype(jnp.bfloat16)


def split_parts(row):
    high = row.astype(jnp.bfloat16)
    rest = row - high.astype(jnp.float32)
    middle = rest.astype(jnp.bfloat16)
    low = (rest - middle.astype(jnp.float32)).astype(jnp.bfloat16)
    return [part.astype(jnp.float32) for part in (high, middle, low)]


def pack_kernel(offsets, key_hbm, value_hbm, hidden_hbm, qgain, kgain, gate, *refs):
    outs, sems = refs[: len(offsets)], refs[len(offsets)]
    rows = key_hbm.shape[0]
    width = outs[0].shape[1]
    half = rows // 2
    tm = lax.axis_index("tm")
    first = pl.multiple_of(lax.axis_index("segment") * half, 16)
    copies = []
    for at, offset in enumerate(offsets):
        column = pl.multiple_of((tm ^ offset) * width, 128)
        columns = pl.ds(column, width)
        moves = (
            (key_hbm.at[:, columns], outs[at].at[pl.ds(0, rows)]),
            (value_hbm.at[:, columns], outs[at].at[pl.ds(rows, rows)]),
            (hidden_hbm.at[pl.ds(first, half), columns], outs[at].at[pl.ds(2 * rows, half)]),
        )
        row = []
        for which, (source, target) in enumerate(moves):
            copy = pltpu.make_async_copy(source, target, sems.at[at, which])
            copy.start()
            row.append(copy)
        copies.append(row)
    gain = kgain[...]
    for at, offset in enumerate(offsets):
        out = outs[at]
        if offset == 0:
            columns = pl.ds(pl.multiple_of(tm * width, 128), width)
            gate_row = gate[:, columns]
            query_row = jnp.concatenate([qgain[...]] * (width // HEAD_DIM), axis=1)
            parts = split_parts(gate_row) + split_parts(query_row)
            index = lax.broadcasted_iota(jnp.int32, (PART_ROWS, width), 0)
            table = jnp.zeros((PART_ROWS, width), jnp.float32)
            for line, part in enumerate(parts):
                table = jnp.where(index == line, part, table)
            out[pl.ds(2 * rows + half, PART_ROWS), :] = table.astype(jnp.bfloat16)
        copies[at][0].wait()
        for head in range(width // HEAD_DIM):
            lanes = pl.ds(head * HEAD_DIM, HEAD_DIM)
            out[pl.ds(0, rows), lanes] = normed(out[pl.ds(0, rows), lanes], gain)
    for row in copies:
        row[1].wait()
        row[2].wait()


def layer_rows(rows, current, keys, values, bias, query_gain, gate):
    scale = 2.0 / math.sqrt(HEAD_DIM) * math.log2(math.e)
    queries = normed(current, query_gain)
    scores = lax.dot_general(
        queries, keys, (((1,), (1,)), ((), ())), preferred_element_type=jnp.float32
    )
    weights = jnp.exp2(scores * scale + bias)
    denominator = jnp.sum(weights, axis=-1, keepdims=True)
    mixture = jnp.dot(weights.astype(jnp.bfloat16), values, preferred_element_type=jnp.float32)
    mixture = mixture / denominator
    return (current.astype(jnp.float32) + gate * mixture).astype(jnp.bfloat16)


def attend_kernel(offsets, rows, key_ids, query_ids, *refs):
    count = len(offsets)
    own, other, outs = refs[:count], refs[count : 2 * count], refs[2 * count : 3 * count]
    bias_ref = refs[3 * count]
    width = outs[0].shape[1]
    half = rows // 2
    core = lax.axis_index("head")
    keys_row, queries_column = key_ids[...], query_ids[...]
    allowed = (keys_row <= queries_column) & (keys_row >= queries_column - 2)
    bias_ref[...] = jnp.where(allowed, 0.0, BLOCKED)

    def run(first, second, last):
        for head in range(width // HEAD_DIM):
            lanes = pl.ds(head * HEAD_DIM, HEAD_DIM)
            bias = bias_ref[...]

            def part(refs_, start, size):
                return jnp.concatenate([ref[pl.ds(start, size), lanes] for ref in refs_], axis=0)

            def table(refs_, line):
                at = offsets.index(0)
                block = refs_[at][pl.ds(2 * rows + half, PART_ROWS), lanes].astype(jnp.float32)
                return block[line : line + 1] + (
                    block[line + 1 : line + 2] + block[line + 2 : line + 3]
                )

            current = jnp.concatenate(
                [ref[pl.ds(2 * rows, half), lanes] for at in range(count) for ref in (first[at], second[at])],
                axis=0,
            )
            for section in range(last + 1):
                source = (first, second)[section]
                current = layer_rows(
                    rows,
                    current,
                    part(source, 0, rows),
                    part(source, rows, rows),
                    bias,
                    table(source, 3),
                    table(source, 0),
                )
            for at in range(count):
                outs[at][:, lanes] = current[at * rows : (at + 1) * rows]

    @pl.when(core == 0)
    def _():
        run(own, other, 0)

    @pl.when(core != 0)
    def _():
        run(other, own, 1)


def join_kernel(offsets, *refs):
    out = refs[len(offsets)]
    width = refs[0].shape[1]
    tm = lax.axis_index("tm")
    for at, offset in enumerate(offsets):
        out[:, pl.ds(pl.multiple_of((tm ^ offset) * width, 128), width)] = refs[at][...]


def by_heads(hidden_in, key_cache, value_cache, query_gain, key_gain, out_gate, span_ids):
    rows, features = hidden_in.shape
    blocks = lax.axis_size("tm")
    width = features // blocks
    half = rows // 2
    tm = lax.axis_index("tm")
    offsets = tuple(sorted(range(blocks), key=lambda k: (k < blocks // 2, k if k >= blocks // 2 else -k)))
    vmem = pl.BlockSpec(memory_space=pltpu.VMEM)
    hbm = pl.BlockSpec(memory_space=pl.ANY)
    sizes = [2 * rows + half + (PART_ROWS if offset == 0 else 0) for offset in offsets]
    payloads = pl.pallas_call(
        functools.partial(pack_kernel, offsets),
        out_shape=[jax.ShapeDtypeStruct((size, width), jnp.bfloat16) for size in sizes],
        in_specs=[hbm, hbm, hbm, vmem, vmem, vmem],
        out_specs=[vmem] * blocks,
        scratch_shapes=[pltpu.SemaphoreType.DMA((blocks, 3))],
        name="pack",
    )(key_cache[0], value_cache[0], hidden_in, query_gain, key_gain, out_gate)
    own = [swapped(payload, offset, blocks) for payload, offset in zip(payloads, offsets)]
    other = [lax.ppermute(payload, "head", [(0, 1), (1, 0)]) for payload in own]
    ids = jnp.concatenate(
        [lax.dynamic_slice_in_dim(span_ids, (tm ^ offset) * rows, rows, 0) for offset in offsets]
    )
    total = rows * blocks
    results = pl.pallas_call(
        functools.partial(attend_kernel, offsets, rows),
        out_shape=[jax.ShapeDtypeStruct((rows, width), jnp.bfloat16)] * blocks,
        in_specs=[vmem] * (2 + 2 * blocks),
        out_specs=[vmem] * blocks,
        scratch_shapes=[pltpu.VMEM((total, total), jnp.float32)],
        name="attend",
    )(ids.reshape(1, total), ids.reshape(total, 1), *own, *other)
    back = [swapped(result, offset, blocks) for result, offset in zip(results, offsets)]
    joined = pl.pallas_call(
        functools.partial(join_kernel, offsets),
        out_shape=jax.ShapeDtypeStruct((rows, features), jnp.bfloat16),
        in_specs=[vmem] * blocks,
        out_specs=vmem,
        name="join",
    )(*back)
    return joined[None]


def solution(mesh):
    placed = (
        P(("groups", "tm"), "head"),
        P("segment", ("groups", "tm"), "head"),
        P("segment", ("groups", "tm"), "head"),
        P("segment", None),
        P("segment", None),
        P("segment", "head"),
        P("groups"),
    )
    blocks = mesh.shape["tm"]
    two_by_two = mesh.shape["segment"] == 2 and mesh.shape["head"] == 2

    def run(hidden_in, *rest):
        rows, features = hidden_in.shape
        fits = features % (blocks * HEAD_DIM) == 0 and rows % 32 == 0
        if two_by_two and blocks & (blocks - 1) == 0 and fits:
            return by_heads(hidden_in, *rest)
        return body(hidden_in, *rest)

    return jax.shard_map(
        run,
        mesh=mesh,
        in_specs=placed,
        out_specs=P("segment", ("groups", "tm"), "head"),
        check_vma=False,
    )
```

```python
import functools
import math

import jax
import jax.numpy as jnp
from jax import lax
from jax.experimental import pallas as pl
from jax.experimental.pallas import tpu as pltpu
from jax.sharding import PartitionSpec as P


HEAD_DIM = 128
PART_ROWS = 16
BLOCKED = -1e30
PACK_GRANT = 54880 << 10


def passed_along(shard, axis, by):
    devices = lax.axis_size(axis)
    pairs = [(i, i + by) for i in range(devices) if 0 <= i + by < devices]
    return lax.ppermute(shard, axis, pairs)


def head_normalize(features, gain_row):
    row_count = features.shape[0]
    shaped = features.astype(jnp.float32).reshape(row_count, -1, HEAD_DIM)
    inverse_rms = lax.rsqrt(jnp.mean(shaped * shaped, axis=-1, keepdims=True) + 1e-06)
    return (shaped * inverse_rms * gain_row).reshape(features.shape).astype(jnp.bfloat16)


def attend_heads(queries, key_rows, value_rows, query_ids, key_ids):
    row_count = queries.shape[0]
    key_count = key_rows.shape[0]
    pair_width = 2 * HEAD_DIM
    group_count = queries.shape[1] // pair_width
    score_scale = 2.0 / math.sqrt(HEAD_DIM)
    allowed = (key_ids[None, :] <= query_ids[:, None]) & (
        key_ids[None, :] >= query_ids[:, None] - 2
    )

    def pair_step(group_index, result):
        column = group_index * pair_width
        query_pair = lax.dynamic_slice_in_dim(queries, column, pair_width, 1).reshape(
            row_count, 2, HEAD_DIM
        )
        key_pair = lax.dynamic_slice_in_dim(key_rows, column, pair_width, 1).reshape(
            key_count, 2, HEAD_DIM
        )
        value_pair = lax.dynamic_slice_in_dim(value_rows, column, pair_width, 1).reshape(
            key_count, 2, HEAD_DIM
        )
        scores = (
            jnp.einsum("rhd,khd->hrk", query_pair, key_pair, preferred_element_type=jnp.float32)
            * score_scale
        )
        weights = jnp.where(allowed[None], jnp.exp(scores), 0.0)
        denominator = jnp.sum(weights, axis=-1)
        mixture = jnp.einsum(
            "hrk,khd->rhd",
            weights.astype(jnp.bfloat16),
            value_pair,
            preferred_element_type=jnp.float32,
        )
        mixture = mixture / jnp.transpose(denominator)[:, :, None]
        return lax.dynamic_update_slice_in_dim(
            result, mixture.reshape(row_count, pair_width), column, 1
        )

    initial = jnp.zeros((row_count, queries.shape[1]), jnp.float32)
    return lax.fori_loop(0, group_count, pair_step, initial)


def body(hidden_in, key_cache, value_cache, query_gain, key_gain, out_gate, span_ids):
    block_rows = hidden_in.shape[0]
    tm_index = lax.axis_index("tm")
    segment_index = lax.axis_index("segment")
    normed_keys = head_normalize(key_cache[0], key_gain[0])
    own_values = value_cache[0]
    first_row = tm_index * block_rows
    all_keys, all_values = (
        lax.all_gather(normed_keys, "tm", axis=0, tiled=True),
        lax.all_gather(own_values, "tm", axis=0, tiled=True),
    )

    def update(row_block):
        queries = head_normalize(row_block, query_gain[0])
        query_ids = lax.dynamic_slice_in_dim(span_ids, first_row, row_block.shape[0], 0)
        mixture = attend_heads(queries, all_keys, all_values, query_ids, span_ids)
        return (row_block.astype(jnp.float32) + out_gate[0] * mixture).astype(jnp.bfloat16)

    segments = lax.axis_size("segment")
    current = hidden_in
    result = hidden_in
    for section in range(segments):
        active = segment_index == section
        produced = lax.cond(active, lambda inputs: update(inputs), lambda inputs: inputs, current)
        result = jnp.where(active, produced, result)
        if section + 1 < segments:
            arrived = passed_along(produced, "segment", 1)
            current = jnp.where(segment_index == section + 1, arrived, current)
    return result[None]


MESH_TAIL = ("tm", "segment", "head")


def swapped(array, offset, blocks):
    at = lambda t, s, c: (t * 2 + s) * 2 + c
    pairs = [
        (at(t, s, c), at(t ^ offset, c, s))
        for t in range(blocks)
        for s in range(2)
        for c in range(2)
    ]
    return lax.ppermute(array, MESH_TAIL, pairs)


def normed(rows, gain):
    rows = rows.astype(jnp.float32)
    inverse_rms = lax.rsqrt(jnp.mean(rows * rows, axis=-1, keepdims=True) + 1e-06)
    return (rows * inverse_rms * gain).astype(jnp.bfloat16)


def split_parts(row):
    high = row.astype(jnp.bfloat16)
    rest = row - high.astype(jnp.float32)
    middle = rest.astype(jnp.bfloat16)
    low = (rest - middle.astype(jnp.float32)).astype(jnp.bfloat16)
    return [part.astype(jnp.float32) for part in (high, middle, low)]


def pack_kernel(offset, key_hbm, value_hbm, hidden_hbm, qgain_hbm, kgain_hbm, gate_hbm, *refs):
    out, kgain, qgain, gate, sems = refs[-5:]
    rows = key_hbm.shape[0]
    width = out.shape[1]
    half = rows // 2
    tm = lax.axis_index("tm")
    first = pl.multiple_of(lax.axis_index("segment") * half, 16)
    columns = pl.ds(pl.multiple_of((tm ^ offset) * width, 128), width)
    moves = [
        (key_hbm.at[:, columns], out.at[pl.ds(0, rows)]),
        (kgain_hbm, kgain),
        (value_hbm.at[:, columns], out.at[pl.ds(rows, rows)]),
        (hidden_hbm.at[pl.ds(first, half), columns], out.at[pl.ds(2 * rows, half)]),
    ]
    if offset == 0:
        moves += [(qgain_hbm, qgain), (gate_hbm.at[:, columns], gate)]
    copies = []
    for which, (source, target) in enumerate(moves):
        copy = pltpu.make_async_copy(source, target, sems.at[which])
        copy.start()
        copies.append(copy)
    copies[0].wait()
    copies[1].wait()
    gain = kgain[...]
    for head in range(width // HEAD_DIM):
        lanes = pl.ds(head * HEAD_DIM, HEAD_DIM)
        out[pl.ds(0, rows), lanes] = normed(out[pl.ds(0, rows), lanes], gain)
    for copy in copies[2:]:
        copy.wait()
    if offset == 0:
        query_row = jnp.concatenate([qgain[...]] * (width // HEAD_DIM), axis=1)
        parts = split_parts(gate[...]) + split_parts(query_row)
        index = lax.broadcasted_iota(jnp.int32, (PART_ROWS, width), 0)
        table = jnp.zeros((PART_ROWS, width), jnp.float32)
        for line, part in enumerate(parts):
            table = jnp.where(index == line, part, table)
        out[pl.ds(2 * rows + half, PART_ROWS), :] = table.astype(jnp.bfloat16)


def layer_rows(current, keys, values, bias, query_gain, gate):
    scale = 2.0 / math.sqrt(HEAD_DIM) * math.log2(math.e)
    queries = normed(current, query_gain)
    scores = lax.dot_general(
        queries, keys, (((1,), (1,)), ((), ())), preferred_element_type=jnp.float32
    )
    weights = jnp.exp2(scores * scale + bias)
    denominator = jnp.sum(weights, axis=-1, keepdims=True)
    mixture = jnp.dot(weights.astype(jnp.bfloat16), values, preferred_element_type=jnp.float32)
    mixture = mixture / denominator
    return (current.astype(jnp.float32) + gate * mixture).astype(jnp.bfloat16)


def attend_kernel(offsets, rows, key_ids, query_ids, *refs):
    count = len(offsets)
    own, other, outs = refs[:count], refs[count : 2 * count], refs[2 * count : 3 * count]
    bias_ref = refs[3 * count]
    width = outs[0].shape[1]
    half = rows // 2
    core = lax.axis_index("head")
    keys_row, queries_column = key_ids[...], query_ids[...]
    allowed = (keys_row <= queries_column) & (keys_row >= queries_column - 2)
    bias_ref[...] = jnp.where(allowed, 0.0, BLOCKED)

    def run(first, second, last):
        for head in range(width // HEAD_DIM):
            lanes = pl.ds(head * HEAD_DIM, HEAD_DIM)
            bias = bias_ref[...]

            def part(refs_, start, size):
                return jnp.concatenate([ref[pl.ds(start, size), lanes] for ref in refs_], axis=0)

            def table(refs_, line):
                at = offsets.index(0)
                block = refs_[at][pl.ds(2 * rows + half, PART_ROWS), lanes].astype(jnp.float32)
                return block[line : line + 1] + (
                    block[line + 1 : line + 2] + block[line + 2 : line + 3]
                )

            current = jnp.concatenate(
                [ref[pl.ds(2 * rows, half), lanes] for at in range(count) for ref in (first[at], second[at])],
                axis=0,
            )
            for section in range(last + 1):
                source = (first, second)[section]
                current = layer_rows(
                    current,
                    part(source, 0, rows),
                    part(source, rows, rows),
                    bias,
                    table(source, 3),
                    table(source, 0),
                )
            for at in range(count):
                outs[at][:, lanes] = current[at * rows : (at + 1) * rows]

    @pl.when(core == 0)
    def _():
        run(own, other, 0)

    @pl.when(core != 0)
    def _():
        run(other, own, 1)


def join_kernel(offsets, *refs):
    out = refs[len(offsets)]
    width = refs[0].shape[1]
    tm = lax.axis_index("tm")
    for at, offset in enumerate(offsets):
        out[:, pl.ds(pl.multiple_of((tm ^ offset) * width, 128), width)] = refs[at][...]


def grant(size):
    return pltpu.CompilerParams(vmem_limit_bytes=size)


def by_heads(hidden_in, key_cache, value_cache, query_gain, key_gain, out_gate, span_ids):
    rows, features = hidden_in.shape
    blocks = lax.axis_size("tm")
    width = features // blocks
    half = rows // 2
    total = rows * blocks
    tm = lax.axis_index("tm")
    offsets = send_order(blocks)
    vmem = pl.BlockSpec(memory_space=pltpu.VMEM)
    hbm = pl.BlockSpec(memory_space=pltpu.HBM)
    anywhere = pl.BlockSpec(memory_space=pl.ANY)

    ids = jnp.concatenate(
        [lax.dynamic_slice_in_dim(span_ids, (tm ^ offset) * rows, rows, 0) for offset in offsets]
    )
    ids_row, ids_column = ids.reshape(1, total), ids.reshape(total, 1)

    def pack(at, *after):
        offset = offsets[at]
        size = 2 * rows + half + (PART_ROWS if offset == 0 else 0)
        payload = pl.pallas_call(
            functools.partial(pack_kernel, offset),
            out_shape=jax.ShapeDtypeStruct((size, width), jnp.bfloat16),
            in_specs=[hbm] * 6 + [anywhere] * len(after),
            out_specs=vmem,
            scratch_shapes=[
                pltpu.VMEM((1, HEAD_DIM), jnp.float32),
                pltpu.VMEM((1, HEAD_DIM), jnp.float32),
                pltpu.VMEM((1, width), jnp.float32),
                pltpu.SemaphoreType.DMA((6,)),
            ],
            compiler_params=grant(PACK_GRANT),
        )(key_cache[0], value_cache[0], hidden_in, query_gain, key_gain, out_gate, *after)
        return payload

    own, other = [], []
    for at, offset in enumerate(offsets):
        payload = pack(at, *((ids_row, ids_column) if at == blocks - 1 else ()))
        own.append(swapped(payload, offset, blocks))
    for payload in own:
        other.append(lax.ppermute(payload, "head", [(0, 1), (1, 0)]))
    results = pl.pallas_call(
        functools.partial(attend_kernel, offsets, rows),
        out_shape=[jax.ShapeDtypeStruct((rows, width), jnp.bfloat16)] * blocks,
        in_specs=[vmem] * (2 + 2 * blocks),
        out_specs=[vmem] * blocks,
        scratch_shapes=[pltpu.VMEM((total, total), jnp.float32)],
        compiler_params=grant(12 << 20),
        name="attend",
    )(ids_row, ids_column, *own, *other)
    back = []
    for at, offset in enumerate(offsets):
        back.append(swapped(results[at], offset, blocks))
    joined = pl.pallas_call(
        functools.partial(join_kernel, offsets),
        out_shape=jax.ShapeDtypeStruct((rows, features), jnp.bfloat16),
        in_specs=[vmem] * blocks,
        out_specs=vmem,
        compiler_params=grant(2 << 20),
        name="join",
    )(*back)
    return joined[None]


def send_order(blocks):
    far = blocks // 2
    return tuple(range(far, blocks)) + tuple(reversed(range(far)))


def solution(mesh):
    placed = (
        P(("groups", "tm"), "head"),
        P("segment", ("groups", "tm"), "head"),
        P("segment", ("groups", "tm"), "head"),
        P("segment", None),
        P("segment", None),
        P("segment", "head"),
        P("groups"),
    )
    blocks = mesh.shape["tm"]
    two_by_two = mesh.shape["segment"] == 2 and mesh.shape["head"] == 2
    mapped = functools.partial(
        jax.shard_map,
        mesh=mesh,
        in_specs=placed,
        out_specs=P("segment", ("groups", "tm"), "head"),
        check_vma=False,
    )

    def run(hidden_in, *rest):
        rows = hidden_in.shape[0] // (mesh.shape["groups"] * blocks)
        features = hidden_in.shape[1] // mesh.shape["head"]
        fits = features % (blocks * HEAD_DIM) == 0 and rows % 32 == 0
        if two_by_two and blocks & (blocks - 1) == 0 and fits:
            step = mapped(by_heads)
        else:
            step = mapped(body)
        return step(hidden_in, *rest)

    return run
```

```python
import functools
import math

import jax
import jax.numpy as jnp
from jax import lax
from jax.experimental import pallas as pl
from jax.experimental.pallas import tpu as pltpu
from jax.sharding import PartitionSpec as P


HEAD_DIM = 128
PART_ROWS = 16
BLOCKED = -1e30


def passed_along(shard, axis, by):
    devices = lax.axis_size(axis)
    pairs = [(i, i + by) for i in range(devices) if 0 <= i + by < devices]
    return lax.ppermute(shard, axis, pairs)


def head_normalize(features, gain_row):
    row_count = features.shape[0]
    shaped = features.astype(jnp.float32).reshape(row_count, -1, HEAD_DIM)
    inverse_rms = lax.rsqrt(jnp.mean(shaped * shaped, axis=-1, keepdims=True) + 1e-06)
    return (shaped * inverse_rms * gain_row).reshape(features.shape).astype(jnp.bfloat16)


def attend_heads(queries, key_rows, value_rows, query_ids, key_ids):
    row_count = queries.shape[0]
    key_count = key_rows.shape[0]
    pair_width = 2 * HEAD_DIM
    group_count = queries.shape[1] // pair_width
    score_scale = 2.0 / math.sqrt(HEAD_DIM)
    allowed = (key_ids[None, :] <= query_ids[:, None]) & (
        key_ids[None, :] >= query_ids[:, None] - 2
    )

    def pair_step(group_index, result):
        column = group_index * pair_width
        query_pair = lax.dynamic_slice_in_dim(queries, column, pair_width, 1).reshape(
            row_count, 2, HEAD_DIM
        )
        key_pair = lax.dynamic_slice_in_dim(key_rows, column, pair_width, 1).reshape(
            key_count, 2, HEAD_DIM
        )
        value_pair = lax.dynamic_slice_in_dim(value_rows, column, pair_width, 1).reshape(
            key_count, 2, HEAD_DIM
        )
        scores = (
            jnp.einsum("rhd,khd->hrk", query_pair, key_pair, preferred_element_type=jnp.float32)
            * score_scale
        )
        weights = jnp.where(allowed[None], jnp.exp(scores), 0.0)
        denominator = jnp.sum(weights, axis=-1)
        mixture = jnp.einsum(
            "hrk,khd->rhd",
            weights.astype(jnp.bfloat16),
            value_pair,
            preferred_element_type=jnp.float32,
        )
        mixture = mixture / jnp.transpose(denominator)[:, :, None]
        return lax.dynamic_update_slice_in_dim(
            result, mixture.reshape(row_count, pair_width), column, 1
        )

    initial = jnp.zeros((row_count, queries.shape[1]), jnp.float32)
    return lax.fori_loop(0, group_count, pair_step, initial)


def body(hidden_in, key_cache, value_cache, query_gain, key_gain, out_gate, span_ids):
    block_rows = hidden_in.shape[0]
    tm_index = lax.axis_index("tm")
    segment_index = lax.axis_index("segment")
    normed_keys = head_normalize(key_cache[0], key_gain[0])
    own_values = value_cache[0]
    first_row = tm_index * block_rows
    all_keys, all_values = (
        lax.all_gather(normed_keys, "tm", axis=0, tiled=True),
        lax.all_gather(own_values, "tm", axis=0, tiled=True),
    )

    def update(row_block):
        queries = head_normalize(row_block, query_gain[0])
        query_ids = lax.dynamic_slice_in_dim(span_ids, first_row, row_block.shape[0], 0)
        mixture = attend_heads(queries, all_keys, all_values, query_ids, span_ids)
        return (row_block.astype(jnp.float32) + out_gate[0] * mixture).astype(jnp.bfloat16)

    segments = lax.axis_size("segment")
    current = hidden_in
    result = hidden_in
    for section in range(segments):
        active = segment_index == section
        produced = lax.cond(active, lambda inputs: update(inputs), lambda inputs: inputs, current)
        result = jnp.where(active, produced, result)
        if section + 1 < segments:
            arrived = passed_along(produced, "segment", 1)
            current = jnp.where(segment_index == section + 1, arrived, current)
    return result[None]


MESH_TAIL = ("tm", "segment", "head")


def swapped(array, offset, blocks):
    at = lambda t, s, c: (t * 2 + s) * 2 + c
    pairs = [
        (at(t, s, c), at(t ^ offset, c, s))
        for t in range(blocks)
        for s in range(2)
        for c in range(2)
    ]
    return lax.ppermute(array, MESH_TAIL, pairs)


def normed(rows, gain):
    rows = rows.astype(jnp.float32)
    inverse_rms = lax.rsqrt(jnp.mean(rows * rows, axis=-1, keepdims=True) + 1e-06)
    return (rows * inverse_rms * gain).astype(jnp.bfloat16)


def split_parts(row):
    high = row.astype(jnp.bfloat16)
    rest = row - high.astype(jnp.float32)
    middle = rest.astype(jnp.bfloat16)
    low = (rest - middle.astype(jnp.float32)).astype(jnp.bfloat16)
    return [part.astype(jnp.float32) for part in (high, middle, low)]


def pack_kernel(offset, key_hbm, value_hbm, hidden_hbm, kgain_hbm, *refs):
    out, kgain, qgain, gate, sems = refs[-5:]
    rows = key_hbm.shape[0]
    width = out.shape[1]
    half = rows // 2
    tm = lax.axis_index("tm")
    first = pl.multiple_of(lax.axis_index("segment") * half, 16)
    columns = pl.ds(pl.multiple_of((tm ^ offset) * width, 128), width)
    moves = [
        (key_hbm.at[:, columns], out.at[pl.ds(0, rows)]),
        (kgain_hbm, kgain),
        (value_hbm.at[:, columns], out.at[pl.ds(rows, rows)]),
        (hidden_hbm.at[pl.ds(first, half), columns], out.at[pl.ds(2 * rows, half)]),
    ]
    if offset == 0:
        moves += [(refs[0], qgain), (refs[1].at[:, columns], gate)]
    copies = []
    for which, (source, target) in enumerate(moves):
        copy = pltpu.make_async_copy(source, target, sems.at[which])
        copy.start()
        copies.append(copy)
    copies[0].wait()
    copies[1].wait()
    gain = kgain[...]
    for head in range(width // HEAD_DIM):
        lanes = pl.ds(head * HEAD_DIM, HEAD_DIM)
        out[pl.ds(0, rows), lanes] = normed(out[pl.ds(0, rows), lanes], gain)
    for copy in copies[2:]:
        copy.wait()
    if offset == 0:
        query_row = jnp.concatenate([qgain[...]] * (width // HEAD_DIM), axis=1)
        parts = split_parts(gate[...]) + split_parts(query_row)
        index = lax.broadcasted_iota(jnp.int32, (PART_ROWS, width), 0)
        table = jnp.zeros((PART_ROWS, width), jnp.float32)
        for line, part in enumerate(parts):
            table = jnp.where(index == line, part, table)
        out[pl.ds(2 * rows + half, PART_ROWS), :] = table.astype(jnp.bfloat16)


def layer_rows(current, keys, values, bias, query_gain, gate):
    scale = 2.0 / math.sqrt(HEAD_DIM) * math.log2(math.e)
    queries = normed(current, query_gain)
    scores = lax.dot_general(
        queries, keys, (((1,), (1,)), ((), ())), preferred_element_type=jnp.float32
    )
    weights = jnp.exp2(scores * scale + bias)
    denominator = jnp.sum(weights, axis=-1, keepdims=True)
    mixture = jnp.dot(weights.astype(jnp.bfloat16), values, preferred_element_type=jnp.float32)
    mixture = mixture / denominator
    return (current.astype(jnp.float32) + gate * mixture).astype(jnp.bfloat16)


def attend_kernel(offsets, rows, key_ids, query_ids, *refs):
    count = len(offsets)
    own, other, outs = refs[:count], refs[count : 2 * count], refs[2 * count : 3 * count]
    bias_ref = refs[3 * count]
    width = outs[0].shape[1]
    half = rows // 2
    core = lax.axis_index("head")
    keys_row, queries_column = key_ids[...], query_ids[...]
    allowed = (keys_row <= queries_column) & (keys_row >= queries_column - 2)
    bias_ref[...] = jnp.where(allowed, 0.0, BLOCKED)

    def run(first, second, last):
        for head in range(width // HEAD_DIM):
            lanes = pl.ds(head * HEAD_DIM, HEAD_DIM)
            bias = bias_ref[...]

            def part(refs_, start, size):
                return jnp.concatenate([ref[pl.ds(start, size), lanes] for ref in refs_], axis=0)

            def table(refs_, line):
                at = offsets.index(0)
                block = refs_[at][pl.ds(2 * rows + half, PART_ROWS), lanes].astype(jnp.float32)
                return block[line : line + 1] + (
                    block[line + 1 : line + 2] + block[line + 2 : line + 3]
                )

            current = jnp.concatenate(
                [ref[pl.ds(2 * rows, half), lanes] for at in range(count) for ref in (first[at], second[at])],
                axis=0,
            )
            for section in range(last + 1):
                source = (first, second)[section]
                current = layer_rows(
                    current,
                    part(source, 0, rows),
                    part(source, rows, rows),
                    bias,
                    table(source, 3),
                    table(source, 0),
                )
            for at in range(count):
                outs[at][:, lanes] = current[at * rows : (at + 1) * rows]

    @pl.when(core == 0)
    def _():
        run(own, other, 0)

    @pl.when(core != 0)
    def _():
        run(other, own, 1)


def join_kernel(offsets, *refs):
    out = refs[len(offsets)]
    width = refs[0].shape[1]
    tm = lax.axis_index("tm")
    for at, offset in enumerate(offsets):
        out[:, pl.ds(pl.multiple_of((tm ^ offset) * width, 128), width)] = refs[at][...]


def grant(size):
    return pltpu.CompilerParams(vmem_limit_bytes=size)


def by_heads(hidden_in, key_cache, value_cache, query_gain, key_gain, out_gate, span_ids):
    rows, features = hidden_in.shape
    blocks = lax.axis_size("tm")
    width = features // blocks
    half = rows // 2
    total = rows * blocks
    tm = lax.axis_index("tm")
    offsets = send_order(blocks)
    vmem = pl.BlockSpec(memory_space=pltpu.VMEM)
    hbm = pl.BlockSpec(memory_space=pltpu.HBM)
    anywhere = pl.BlockSpec(memory_space=pl.ANY)

    ids = jnp.concatenate(
        [lax.dynamic_slice_in_dim(span_ids, (tm ^ offset) * rows, rows, 0) for offset in offsets]
    )
    ids_row, ids_column = ids.reshape(1, total), ids.reshape(total, 1)

    def pack(at, *after):
        offset = offsets[at]
        size = 2 * rows + half + (PART_ROWS if offset == 0 else 0)
        sources = [key_cache[0], value_cache[0], hidden_in, key_gain]
        if offset == 0:
            sources += [query_gain, out_gate]
        sources = [pltpu.with_memory_space_constraint(source, pltpu.HBM) for source in sources]
        payload = pl.pallas_call(
            functools.partial(pack_kernel, offset),
            out_shape=jax.ShapeDtypeStruct((size, width), jnp.bfloat16),
            in_specs=[hbm] * len(sources) + [anywhere] * len(after),
            out_specs=vmem,
            scratch_shapes=[
                pltpu.VMEM((1, HEAD_DIM), jnp.float32),
                pltpu.VMEM((1, HEAD_DIM), jnp.float32),
                pltpu.VMEM((1, width), jnp.float32),
                pltpu.SemaphoreType.DMA((6,)),
            ],
            compiler_params=grant(2 << 20),
        )(*sources, *after)
        return payload

    own, other = [], []
    for at, offset in enumerate(offsets):
        payload = pack(at, *((ids_row, ids_column) if at == blocks - 1 else ()))
        own.append(swapped(payload, offset, blocks))
    for payload in own:
        other.append(lax.ppermute(payload, "head", [(0, 1), (1, 0)]))
    results = pl.pallas_call(
        functools.partial(attend_kernel, offsets, rows),
        out_shape=[jax.ShapeDtypeStruct((rows, width), jnp.bfloat16)] * blocks,
        in_specs=[vmem] * (2 + 2 * blocks),
        out_specs=[vmem] * blocks,
        scratch_shapes=[pltpu.VMEM((total, total), jnp.float32)],
        compiler_params=grant(12 << 20),
        name="attend",
    )(ids_row, ids_column, *own, *other)
    back = []
    for at, offset in enumerate(offsets):
        back.append(swapped(results[at], offset, blocks))
    joined = pl.pallas_call(
        functools.partial(join_kernel, offsets),
        out_shape=jax.ShapeDtypeStruct((rows, features), jnp.bfloat16),
        in_specs=[vmem] * blocks,
        out_specs=vmem,
        compiler_params=grant(2 << 20),
        name="join",
    )(*back)
    return joined[None]


def send_order(blocks):
    far = blocks // 2
    return (far, *range(1, far), *range(far + 1, blocks), 0)


def solution(mesh):
    placed = (
        P(("groups", "tm"), "head"),
        P("segment", ("groups", "tm"), "head"),
        P("segment", ("groups", "tm"), "head"),
        P("segment", None),
        P("segment", None),
        P("segment", "head"),
        P("groups"),
    )
    blocks = mesh.shape["tm"]
    two_by_two = mesh.shape["segment"] == 2 and mesh.shape["head"] == 2
    mapped = functools.partial(
        jax.shard_map,
        mesh=mesh,
        in_specs=placed,
        out_specs=P("segment", ("groups", "tm"), "head"),
        check_vma=False,
    )

    def run(hidden_in, *rest):
        rows = hidden_in.shape[0] // (mesh.shape["groups"] * blocks)
        features = hidden_in.shape[1] // mesh.shape["head"]
        fits = features % (blocks * HEAD_DIM) == 0 and rows % 32 == 0
        if two_by_two and blocks & (blocks - 1) == 0 and fits:
            step = mapped(by_heads)
        else:
            step = mapped(body)
        return step(hidden_in, *rest)

    return run
```

```python
import functools
import math

import jax
import jax.numpy as jnp
from jax import lax
from jax.experimental import pallas as pl
from jax.experimental.pallas import tpu as pltpu
from jax.sharding import PartitionSpec as P


HEAD_DIM = 128
PART_ROWS = 16
BLOCKED = -1e30


def passed_along(shard, axis, by):
    devices = lax.axis_size(axis)
    pairs = [(i, i + by) for i in range(devices) if 0 <= i + by < devices]
    return lax.ppermute(shard, axis, pairs)


def head_normalize(features, gain_row):
    row_count = features.shape[0]
    shaped = features.astype(jnp.float32).reshape(row_count, -1, HEAD_DIM)
    inverse_rms = lax.rsqrt(jnp.mean(shaped * shaped, axis=-1, keepdims=True) + 1e-06)
    return (shaped * inverse_rms * gain_row).reshape(features.shape).astype(jnp.bfloat16)


def attend_heads(queries, key_rows, value_rows, query_ids, key_ids):
    row_count = queries.shape[0]
    key_count = key_rows.shape[0]
    pair_width = 2 * HEAD_DIM
    group_count = queries.shape[1] // pair_width
    score_scale = 2.0 / math.sqrt(HEAD_DIM)
    allowed = (key_ids[None, :] <= query_ids[:, None]) & (
        key_ids[None, :] >= query_ids[:, None] - 2
    )

    def pair_step(group_index, result):
        column = group_index * pair_width
        query_pair = lax.dynamic_slice_in_dim(queries, column, pair_width, 1).reshape(
            row_count, 2, HEAD_DIM
        )
        key_pair = lax.dynamic_slice_in_dim(key_rows, column, pair_width, 1).reshape(
            key_count, 2, HEAD_DIM
        )
        value_pair = lax.dynamic_slice_in_dim(value_rows, column, pair_width, 1).reshape(
            key_count, 2, HEAD_DIM
        )
        scores = (
            jnp.einsum("rhd,khd->hrk", query_pair, key_pair, preferred_element_type=jnp.float32)
            * score_scale
        )
        weights = jnp.where(allowed[None], jnp.exp(scores), 0.0)
        denominator = jnp.sum(weights, axis=-1)
        mixture = jnp.einsum(
            "hrk,khd->rhd",
            weights.astype(jnp.bfloat16),
            value_pair,
            preferred_element_type=jnp.float32,
        )
        mixture = mixture / jnp.transpose(denominator)[:, :, None]
        return lax.dynamic_update_slice_in_dim(
            result, mixture.reshape(row_count, pair_width), column, 1
        )

    initial = jnp.zeros((row_count, queries.shape[1]), jnp.float32)
    return lax.fori_loop(0, group_count, pair_step, initial)


def body(hidden_in, key_cache, value_cache, query_gain, key_gain, out_gate, span_ids):
    block_rows = hidden_in.shape[0]
    tm_index = lax.axis_index("tm")
    segment_index = lax.axis_index("segment")
    normed_keys = head_normalize(key_cache[0], key_gain[0])
    own_values = value_cache[0]
    first_row = tm_index * block_rows
    all_keys, all_values = (
        lax.all_gather(normed_keys, "tm", axis=0, tiled=True),
        lax.all_gather(own_values, "tm", axis=0, tiled=True),
    )

    def update(row_block):
        queries = head_normalize(row_block, query_gain[0])
        query_ids = lax.dynamic_slice_in_dim(span_ids, first_row, row_block.shape[0], 0)
        mixture = attend_heads(queries, all_keys, all_values, query_ids, span_ids)
        return (row_block.astype(jnp.float32) + out_gate[0] * mixture).astype(jnp.bfloat16)

    segments = lax.axis_size("segment")
    current = hidden_in
    result = hidden_in
    for section in range(segments):
        active = segment_index == section
        produced = lax.cond(active, lambda inputs: update(inputs), lambda inputs: inputs, current)
        result = jnp.where(active, produced, result)
        if section + 1 < segments:
            arrived = passed_along(produced, "segment", 1)
            current = jnp.where(segment_index == section + 1, arrived, current)
    return result[None]


MESH_TAIL = ("tm", "segment", "head")


def swapped(array, offset, blocks, own=True):
    at = lambda t, s, c: (t * 2 + s) * 2 + c
    pairs = [
        (at(t, s, c), at(t ^ offset, c, s))
        for t in range(blocks)
        for s in range(2)
        for c in range(2)
        if own or offset or s != c
    ]
    return lax.ppermute(array, MESH_TAIL, pairs)


def normed(rows, gain):
    rows = rows.astype(jnp.float32)
    inverse_rms = lax.rsqrt(jnp.mean(rows * rows, axis=-1, keepdims=True) + 1e-06)
    return (rows * inverse_rms * gain).astype(jnp.bfloat16)


def split_parts(row):
    high = row.astype(jnp.bfloat16)
    rest = row - high.astype(jnp.float32)
    middle = rest.astype(jnp.bfloat16)
    low = (rest - middle.astype(jnp.float32)).astype(jnp.bfloat16)
    return [part.astype(jnp.float32) for part in (high, middle, low)]


def pack_kernel(offset, key_hbm, value_hbm, hidden_hbm, kgain_hbm, *refs):
    out, kgain, qgain, gate, sems = refs[-5:]
    rows = key_hbm.shape[0]
    width = out.shape[1]
    half = rows // 2
    tm = lax.axis_index("tm")
    first = pl.multiple_of(lax.axis_index("segment") * half, 16)
    columns = pl.ds(pl.multiple_of((tm ^ offset) * width, 128), width)
    moves = [
        (key_hbm.at[:, columns], out.at[pl.ds(0, rows)]),
        (kgain_hbm, kgain),
        (value_hbm.at[:, columns], out.at[pl.ds(rows, rows)]),
        (hidden_hbm.at[pl.ds(first, half), columns], out.at[pl.ds(2 * rows, half)]),
    ]
    if offset == 0:
        moves += [(refs[0], qgain), (refs[1].at[:, columns], gate)]
    copies = []
    for which, (source, target) in enumerate(moves):
        copy = pltpu.make_async_copy(source, target, sems.at[which])
        copy.start()
        copies.append(copy)
    copies[0].wait()
    copies[1].wait()
    gain = kgain[...]
    for head in range(width // HEAD_DIM):
        lanes = pl.ds(head * HEAD_DIM, HEAD_DIM)
        out[pl.ds(0, rows), lanes] = normed(out[pl.ds(0, rows), lanes], gain)
    for copy in copies[2:]:
        copy.wait()
    if offset == 0:
        query_row = jnp.concatenate([qgain[...]] * (width // HEAD_DIM), axis=1)
        parts = split_parts(gate[...]) + split_parts(query_row)
        index = lax.broadcasted_iota(jnp.int32, (PART_ROWS, width), 0)
        table = jnp.zeros((PART_ROWS, width), jnp.float32)
        for line, part in enumerate(parts):
            table = jnp.where(index == line, part, table)
        out[pl.ds(2 * rows + half, PART_ROWS), :] = table.astype(jnp.bfloat16)


def mask_kernel(key_ids, query_ids, bias):
    keys_row, queries_column = key_ids[...], query_ids[...]
    allowed = (keys_row <= queries_column) & (keys_row >= queries_column - 2)
    bias[...] = jnp.where(allowed, 0.0, BLOCKED)


def layer_rows(current, keys, values, bias, query_gain, gate):
    scale = 2.0 / math.sqrt(HEAD_DIM) * math.log2(math.e)
    queries = normed(current, query_gain)
    scores = lax.dot_general(
        queries, keys, (((1,), (1,)), ((), ())), preferred_element_type=jnp.float32
    )
    weights = jnp.exp2(scores * scale + bias)
    denominator = jnp.sum(weights, axis=-1, keepdims=True)
    mixture = jnp.dot(weights.astype(jnp.bfloat16), values, preferred_element_type=jnp.float32)
    mixture = mixture / denominator
    return (current.astype(jnp.float32) + gate * mixture).astype(jnp.bfloat16)


def attend_kernel(offsets, rows, *refs):
    count = len(offsets)
    bias_ref, refs = refs[0], refs[1:]
    own, other, outs = refs[:count], refs[count : 2 * count], refs[2 * count : 3 * count]
    width = outs[0].shape[1]
    half = rows // 2

    def run(first, second, last):
        def part(refs_, start, size, lanes):
            return jnp.concatenate([ref[pl.ds(start, size), lanes] for ref in refs_], axis=0)

        def table(refs_, line, lanes):
            block = refs_[offsets.index(0)][pl.ds(2 * rows + half, PART_ROWS), lanes]
            block = block.astype(jnp.float32)
            return block[line : line + 1] + (
                block[line + 1 : line + 2] + block[line + 2 : line + 3]
            )

        heads = range(width // HEAD_DIM)
        lanes_of = [pl.ds(head * HEAD_DIM, HEAD_DIM) for head in heads]
        current = [
            jnp.concatenate(
                [
                    ref[pl.ds(2 * rows, half), lanes]
                    for at in range(count)
                    for ref in (first[at], second[at])
                ],
                axis=0,
            )
            for lanes in lanes_of
        ]
        bias = bias_ref[...]
        for section in range(last + 1):
            source = (first, second)[section]
            for head in heads:
                lanes = lanes_of[head]
                current[head] = layer_rows(
                    current[head],
                    part(source, 0, rows, lanes),
                    part(source, rows, rows, lanes),
                    bias,
                    table(source, 3, lanes),
                    table(source, 0, lanes),
                )
        for head in heads:
            for at in range(count):
                outs[at][:, lanes_of[head]] = current[head][at * rows : (at + 1) * rows]

    core = lax.axis_index("head")

    @pl.when(core == 0)
    def _():
        run(own, other, 0)

    @pl.when(core != 0)
    def _():
        run(other, own, 1)


def join_kernel(offsets, kept, *refs):
    blocks, out, sems = refs[:-2], refs[-2], refs[-1]
    width = blocks[0].shape[1]
    tm = lax.axis_index("tm")
    stayed = lax.axis_index("segment") == lax.axis_index("head")
    copies = []
    for at, offset in enumerate(offsets):
        target = out.at[:, pl.ds(pl.multiple_of((tm ^ offset) * width, 128), width)]
        copy = pltpu.make_async_copy(blocks[at], target, sems.at[at])
        copies.append(copy)
        if offset == 0:
            mine = pltpu.make_async_copy(kept, target, sems.at[at])

            @pl.when(stayed)
            def _():
                mine.start()

            @pl.when(jnp.logical_not(stayed))
            def _():
                copy.start()

        else:
            copy.start()
    for copy in copies:
        copy.wait()


def grant(size):
    return pltpu.CompilerParams(vmem_limit_bytes=size)


def by_heads(hidden_in, key_cache, value_cache, query_gain, key_gain, out_gate, span_ids):
    rows, features = hidden_in.shape
    blocks = lax.axis_size("tm")
    width = features // blocks
    half = rows // 2
    total = rows * blocks
    tm = lax.axis_index("tm")
    offsets = send_order(blocks)
    vmem = pl.BlockSpec(memory_space=pltpu.VMEM)
    hbm = pl.BlockSpec(memory_space=pltpu.HBM)
    anywhere = pl.BlockSpec(memory_space=pl.ANY)

    ids = jnp.concatenate(
        [lax.dynamic_slice_in_dim(span_ids, (tm ^ offset) * rows, rows, 0) for offset in offsets]
    )
    bias = pl.pallas_call(
        mask_kernel,
        out_shape=jax.ShapeDtypeStruct((total, total), jnp.float32),
        in_specs=[vmem, vmem],
        out_specs=vmem,
        compiler_params=grant(4 << 20),
        name="mask",
    )(ids.reshape(1, total), ids.reshape(total, 1))

    def pack(at, *after):
        offset = offsets[at]
        size = 2 * rows + half + (PART_ROWS if offset == 0 else 0)
        sources = [key_cache[0], value_cache[0], hidden_in, key_gain]
        if offset == 0:
            sources += [query_gain, out_gate]
        sources = [pltpu.with_memory_space_constraint(source, pltpu.HBM) for source in sources]
        payload = pl.pallas_call(
            functools.partial(pack_kernel, offset),
            out_shape=jax.ShapeDtypeStruct((size, width), jnp.bfloat16),
            in_specs=[hbm] * len(sources) + [anywhere] * len(after),
            out_specs=vmem,
            scratch_shapes=[
                pltpu.VMEM((1, HEAD_DIM), jnp.float32),
                pltpu.VMEM((1, HEAD_DIM), jnp.float32),
                pltpu.VMEM((1, width), jnp.float32),
                pltpu.SemaphoreType.DMA((6,)),
            ],
            compiler_params=grant(2 << 20),
        )(*sources, *after)
        return payload

    own, other = [], []
    for at, offset in enumerate(offsets):
        payload = pack(at, *((bias,) if at == blocks - 1 else ()))
        own.append(swapped(payload, offset, blocks))
    for payload in own:
        other.append(lax.ppermute(payload, "head", [(0, 1), (1, 0)]))
    results = pl.pallas_call(
        functools.partial(attend_kernel, offsets, rows),
        out_shape=[jax.ShapeDtypeStruct((rows, width), jnp.bfloat16)] * blocks,
        in_specs=[vmem] * (1 + 2 * blocks),
        out_specs=[vmem] * blocks,
        compiler_params=grant(12 << 20),
        name="attend",
    )(bias, *own, *other)
    back = {}
    for offset in return_order(blocks):
        result = results[offsets.index(offset)]
        back[offset] = swapped(result, offset, blocks, own=False)
    joined = pl.pallas_call(
        functools.partial(join_kernel, offsets),
        out_shape=jax.ShapeDtypeStruct((rows, features), jnp.bfloat16),
        in_specs=[vmem] * (1 + blocks),
        out_specs=anywhere,
        scratch_shapes=[pltpu.SemaphoreType.DMA((blocks,))],
        compiler_params=grant(2 << 20),
        name="join",
    )(results[offsets.index(0)], *[back[offset] for offset in offsets])
    return joined[None]


def send_order(blocks):
    far = blocks // 2
    return (far, *range(1, far), *range(far + 1, blocks), 0)


def return_order(blocks):
    far = blocks // 2
    return (*range(far, blocks), *reversed(range(far)))


def solution(mesh):
    placed = (
        P(("groups", "tm"), "head"),
        P("segment", ("groups", "tm"), "head"),
        P("segment", ("groups", "tm"), "head"),
        P("segment", None),
        P("segment", None),
        P("segment", "head"),
        P("groups"),
    )
    blocks = mesh.shape["tm"]
    two_by_two = mesh.shape["segment"] == 2 and mesh.shape["head"] == 2
    mapped = functools.partial(
        jax.shard_map,
        mesh=mesh,
        in_specs=placed,
        out_specs=P("segment", ("groups", "tm"), "head"),
        check_vma=False,
    )

    def run(hidden_in, *rest):
        rows = hidden_in.shape[0] // (mesh.shape["groups"] * blocks)
        features = hidden_in.shape[1] // mesh.shape["head"]
        fits = features % (blocks * HEAD_DIM) == 0 and rows % 32 == 0
        if two_by_two and blocks & (blocks - 1) == 0 and fits:
            step = mapped(by_heads)
        else:
            step = mapped(body)
        return step(hidden_in, *rest)

    return run
```

```python
import functools
import math

import jax
import jax.numpy as jnp
from jax import lax
from jax.experimental import pallas as pl
from jax.experimental.pallas import tpu as pltpu
from jax.sharding import PartitionSpec as P


HEAD_DIM = 128
PART_ROWS = 16
BLOCKED = -1e30


def passed_along(shard, axis, by):
    devices = lax.axis_size(axis)
    pairs = [(i, i + by) for i in range(devices) if 0 <= i + by < devices]
    return lax.ppermute(shard, axis, pairs)


def head_normalize(features, gain_row):
    row_count = features.shape[0]
    shaped = features.astype(jnp.float32).reshape(row_count, -1, HEAD_DIM)
    inverse_rms = lax.rsqrt(jnp.mean(shaped * shaped, axis=-1, keepdims=True) + 1e-06)
    return (shaped * inverse_rms * gain_row).reshape(features.shape).astype(jnp.bfloat16)


def attend_heads(queries, key_rows, value_rows, query_ids, key_ids):
    row_count = queries.shape[0]
    key_count = key_rows.shape[0]
    pair_width = 2 * HEAD_DIM
    group_count = queries.shape[1] // pair_width
    score_scale = 2.0 / math.sqrt(HEAD_DIM)
    allowed = (key_ids[None, :] <= query_ids[:, None]) & (
        key_ids[None, :] >= query_ids[:, None] - 2
    )

    def pair_step(group_index, result):
        column = group_index * pair_width
        query_pair = lax.dynamic_slice_in_dim(queries, column, pair_width, 1).reshape(
            row_count, 2, HEAD_DIM
        )
        key_pair = lax.dynamic_slice_in_dim(key_rows, column, pair_width, 1).reshape(
            key_count, 2, HEAD_DIM
        )
        value_pair = lax.dynamic_slice_in_dim(value_rows, column, pair_width, 1).reshape(
            key_count, 2, HEAD_DIM
        )
        scores = (
            jnp.einsum("rhd,khd->hrk", query_pair, key_pair, preferred_element_type=jnp.float32)
            * score_scale
        )
        weights = jnp.where(allowed[None], jnp.exp(scores), 0.0)
        denominator = jnp.sum(weights, axis=-1)
        mixture = jnp.einsum(
            "hrk,khd->rhd",
            weights.astype(jnp.bfloat16),
            value_pair,
            preferred_element_type=jnp.float32,
        )
        mixture = mixture / jnp.transpose(denominator)[:, :, None]
        return lax.dynamic_update_slice_in_dim(
            result, mixture.reshape(row_count, pair_width), column, 1
        )

    initial = jnp.zeros((row_count, queries.shape[1]), jnp.float32)
    return lax.fori_loop(0, group_count, pair_step, initial)


def body(hidden_in, key_cache, value_cache, query_gain, key_gain, out_gate, span_ids):
    block_rows = hidden_in.shape[0]
    tm_index = lax.axis_index("tm")
    segment_index = lax.axis_index("segment")
    normed_keys = head_normalize(key_cache[0], key_gain[0])
    own_values = value_cache[0]
    first_row = tm_index * block_rows
    all_keys, all_values = (
        lax.all_gather(normed_keys, "tm", axis=0, tiled=True),
        lax.all_gather(own_values, "tm", axis=0, tiled=True),
    )

    def update(row_block):
        queries = head_normalize(row_block, query_gain[0])
        query_ids = lax.dynamic_slice_in_dim(span_ids, first_row, row_block.shape[0], 0)
        mixture = attend_heads(queries, all_keys, all_values, query_ids, span_ids)
        return (row_block.astype(jnp.float32) + out_gate[0] * mixture).astype(jnp.bfloat16)

    segments = lax.axis_size("segment")
    current = hidden_in
    result = hidden_in
    for section in range(segments):
        active = segment_index == section
        produced = lax.cond(active, lambda inputs: update(inputs), lambda inputs: inputs, current)
        result = jnp.where(active, produced, result)
        if section + 1 < segments:
            arrived = passed_along(produced, "segment", 1)
            current = jnp.where(segment_index == section + 1, arrived, current)
    return result[None]


MESH_TAIL = ("tm", "segment", "head")


def swapped(array, offset, blocks, own=True):
    at = lambda t, s, c: (t * 2 + s) * 2 + c
    pairs = [
        (at(t, s, c), at(t ^ offset, c, s))
        for t in range(blocks)
        for s in range(2)
        for c in range(2)
        if own or offset or s != c
    ]
    return lax.ppermute(array, MESH_TAIL, pairs)


def normed(rows, gain):
    rows = rows.astype(jnp.float32)
    inverse_rms = lax.rsqrt(jnp.mean(rows * rows, axis=-1, keepdims=True) + 1e-06)
    return (rows * inverse_rms * gain).astype(jnp.bfloat16)


def split_parts(row):
    high = row.astype(jnp.bfloat16)
    rest = row - high.astype(jnp.float32)
    middle = rest.astype(jnp.bfloat16)
    low = (rest - middle.astype(jnp.float32)).astype(jnp.bfloat16)
    return [part.astype(jnp.float32) for part in (high, middle, low)]


def pack_kernel(pieces, width, key_hbm, value_hbm, hidden_hbm, qgain_hbm, kgain_hbm, gate_hbm, *refs):
    outs, (kgain, qgain, gate, sems) = refs[: len(pieces)], refs[len(pieces) :]
    rows = key_hbm.shape[0]
    half = rows // 2
    tm = lax.axis_index("tm")
    first = pl.multiple_of(lax.axis_index("segment") * half, 16)
    taken = 0

    def start(source, target):
        nonlocal taken
        copy = pltpu.make_async_copy(source, target, sems.at[taken])
        taken += 1
        copy.start()
        return copy

    copies = []
    for out, (offset, head) in zip(outs, pieces):
        base = (tm ^ offset) * width + head * HEAD_DIM
        columns = pl.ds(pl.multiple_of(base, 128), out.shape[1])
        row = [start(key_hbm.at[:, columns], out.at[pl.ds(0, rows)])]
        if not copies:
            row.append(start(kgain_hbm, kgain))
        row += [
            start(value_hbm.at[:, columns], out.at[pl.ds(rows, rows)]),
            start(hidden_hbm.at[pl.ds(first, half), columns], out.at[pl.ds(2 * rows, half)]),
        ]
        if offset == 0:
            row += [start(qgain_hbm, qgain), start(gate_hbm.at[:, columns], gate)]
        copies.append(row)
    for at, (out, (offset, _)) in enumerate(zip(outs, pieces)):
        copies[at][0].wait()
        if at == 0:
            copies[at].pop(1).wait()
        gain = kgain[...]
        for head in range(out.shape[1] // HEAD_DIM):
            lanes = pl.ds(head * HEAD_DIM, HEAD_DIM)
            out[pl.ds(0, rows), lanes] = normed(out[pl.ds(0, rows), lanes], gain)
        for copy in copies[at][1:]:
            copy.wait()
        if offset == 0:
            query_row = jnp.concatenate([qgain[...]] * (width // HEAD_DIM), axis=1)
            parts = split_parts(gate[...]) + split_parts(query_row)
            index = lax.broadcasted_iota(jnp.int32, (PART_ROWS, width), 0)
            table = jnp.zeros((PART_ROWS, width), jnp.float32)
            for line, part in enumerate(parts):
                table = jnp.where(index == line, part, table)
            out[pl.ds(2 * rows + half, PART_ROWS), :] = table.astype(jnp.bfloat16)


def mask_kernel(key_ids, query_ids, bias):
    keys_row, queries_column = key_ids[...], query_ids[...]
    allowed = (keys_row <= queries_column) & (keys_row >= queries_column - 2)
    bias[...] = jnp.where(allowed, 0.0, BLOCKED)


def layer_rows(current, keys, values, bias, query_gain, gate):
    scale = 2.0 / math.sqrt(HEAD_DIM) * math.log2(math.e)
    queries = normed(current, query_gain)
    scores = lax.dot_general(
        queries, keys, (((1,), (1,)), ((), ())), preferred_element_type=jnp.float32
    )
    weights = jnp.exp2(scores * scale + bias)
    denominator = jnp.sum(weights, axis=-1, keepdims=True)
    mixture = jnp.dot(weights.astype(jnp.bfloat16), values, preferred_element_type=jnp.float32)
    mixture = mixture / denominator
    return (current.astype(jnp.float32) + gate * mixture).astype(jnp.bfloat16)


def attend_kernel(offsets, rows, heads, bases, *refs):
    count = len(offsets)
    bias_ref, own, other, outs = refs[0], refs[1 : 1 + count], refs[1 + count : 1 + 2 * count], refs[-count:]
    half = rows // 2

    def run(first, second, last):
        def lanes(at, head):
            return pl.ds((head - bases[at]) * HEAD_DIM, HEAD_DIM)

        def part(source, start, head):
            return jnp.concatenate(
                [ref[pl.ds(start, rows), lanes(at, head)] for at, ref in enumerate(source)], axis=0
            )

        def table(source, line, head):
            at = offsets.index(0)
            block = source[at][pl.ds(2 * rows + half, PART_ROWS), lanes(at, head)]
            block = block.astype(jnp.float32)
            return block[line : line + 1] + (
                block[line + 1 : line + 2] + block[line + 2 : line + 3]
            )

        current = {
            head: jnp.concatenate(
                [
                    ref[pl.ds(2 * rows, half), lanes(at, head)]
                    for at in range(count)
                    for ref in (first[at], second[at])
                ],
                axis=0,
            )
            for head in heads
        }
        bias = bias_ref[...]
        for section in range(last + 1):
            source = (first, second)[section]
            for head in heads:
                current[head] = layer_rows(
                    current[head],
                    part(source, 0, head),
                    part(source, rows, head),
                    bias,
                    table(source, 3, head),
                    table(source, 0, head),
                )
        for head in heads:
            columns = pl.ds(head * HEAD_DIM, HEAD_DIM)
            for at in range(count):
                outs[at][:, columns] = current[head][at * rows : (at + 1) * rows]

    core = lax.axis_index("head")

    @pl.when(core == 0)
    def _():
        run(own, other, 0)

    @pl.when(core != 0)
    def _():
        run(other, own, 1)


def join_kernel(offsets, kept, *refs):
    blocks, out, sems = refs[:-2], refs[-2], refs[-1]
    width = blocks[0].shape[1]
    tm = lax.axis_index("tm")
    stayed = lax.axis_index("segment") == lax.axis_index("head")
    copies = []
    for at, offset in enumerate(offsets):
        target = out.at[:, pl.ds(pl.multiple_of((tm ^ offset) * width, 128), width)]
        copy = pltpu.make_async_copy(blocks[at], target, sems.at[at])
        copies.append(copy)
        if offset == 0:
            mine = pltpu.make_async_copy(kept, target, sems.at[at])

            @pl.when(stayed)
            def _():
                mine.start()

            @pl.when(jnp.logical_not(stayed))
            def _():
                copy.start()

        else:
            copy.start()
    for copy in copies:
        copy.wait()


def grant(size):
    return pltpu.CompilerParams(vmem_limit_bytes=size)


def by_heads(hidden_in, key_cache, value_cache, query_gain, key_gain, out_gate, span_ids):
    rows, features = hidden_in.shape
    blocks = lax.axis_size("tm")
    width = features // blocks
    half = rows // 2
    total = rows * blocks
    tm = lax.axis_index("tm")
    vmem = pl.BlockSpec(memory_space=pltpu.VMEM)
    hbm = pl.BlockSpec(memory_space=pltpu.HBM)
    anywhere = pl.BlockSpec(memory_space=pl.ANY)

    count = width // HEAD_DIM
    groups = [(0, count - 1), (count - 1, 1)] if count > 1 else [(0, 1)]
    sends = send_order(blocks, len(groups))
    offsets = tuple(dict.fromkeys(offset for offset, _ in sends))
    late = sends[-1][0]

    sources = [key_cache[0], value_cache[0], hidden_in, query_gain, key_gain, out_gate]
    sources = [pltpu.with_memory_space_constraint(source, pltpu.HBM) for source in sources]

    def pack(chosen):
        shapes = [
            jax.ShapeDtypeStruct(
                (
                    2 * rows + half + (PART_ROWS if offset == 0 else 0),
                    groups[piece][1] * HEAD_DIM if offset == late else width,
                ),
                jnp.bfloat16,
            )
            for offset, piece in chosen
        ]
        heads = [(offset, groups[piece][0] if offset == late else 0) for offset, piece in chosen]
        return pl.pallas_call(
            functools.partial(pack_kernel, tuple(heads), width),
            out_shape=shapes,
            in_specs=[hbm] * len(sources),
            out_specs=[vmem] * len(shapes),
            scratch_shapes=[
                pltpu.VMEM((1, HEAD_DIM), jnp.float32),
                pltpu.VMEM((1, HEAD_DIM), jnp.float32),
                pltpu.VMEM((1, width), jnp.float32),
                pltpu.SemaphoreType.DMA((3 * len(shapes) + 3,)),
            ],
            compiler_params=grant(4 << 20),
        )(*sources)

    payloads = [*pack(sends[:1]), *pack(sends[1:])]
    own, other = {}, {}
    for key, payload in zip(sends, payloads):
        own[key] = swapped(payload, key[0], blocks)
        other[key] = lax.ppermute(own[key], "head", [(0, 1), (1, 0)])

    ids = jnp.concatenate(
        [lax.dynamic_slice_in_dim(span_ids, (tm ^ offset) * rows, rows, 0) for offset in offsets]
    )
    bias = pl.pallas_call(
        mask_kernel,
        out_shape=jax.ShapeDtypeStruct((total, total), jnp.float32),
        in_specs=[vmem, vmem],
        out_specs=vmem,
        compiler_params=grant(4 << 20),
        name="mask",
    )(ids.reshape(1, total), ids.reshape(total, 1))

    results = []
    for group, (start, heads) in enumerate(groups):
        chosen = [(offset, group if offset == late else 0) for offset in offsets]
        bases = tuple(start if offset == late else 0 for offset in offsets)
        operands = [bias, *[own[key] for key in chosen], *[other[key] for key in chosen], *results]
        results = pl.pallas_call(
            functools.partial(
                attend_kernel, offsets, rows, tuple(range(start, start + heads)), bases
            ),
            out_shape=[jax.ShapeDtypeStruct((rows, width), jnp.bfloat16)] * blocks,
            in_specs=[vmem] * len(operands),
            out_specs=[vmem] * blocks,
            input_output_aliases={1 + 2 * blocks + at: at for at in range(len(results))},
            compiler_params=grant(8 << 20),
        )(*operands)
    back = {}
    for offset in return_order(blocks):
        result = results[offsets.index(offset)]
        back[offset] = swapped(result, offset, blocks, own=False)
    joined = pl.pallas_call(
        functools.partial(join_kernel, offsets),
        out_shape=jax.ShapeDtypeStruct((rows, features), jnp.bfloat16),
        in_specs=[vmem] * (1 + blocks),
        out_specs=anywhere,
        scratch_shapes=[pltpu.SemaphoreType.DMA((blocks,))],
        compiler_params=grant(2 << 20),
        name="join",
    )(results[offsets.index(0)], *[back[offset] for offset in offsets])
    return joined[None]


def send_order(blocks, pieces):
    far = blocks // 2
    late = blocks - 1
    whole = [offset for offset in (far, *range(1, far), *range(far + 1, blocks)) if offset != late]
    split = [(late, piece) for piece in range(pieces)]
    return (*[(offset, 0) for offset in whole], *split[:-1], (0, 0), split[-1])


def return_order(blocks):
    far = blocks // 2
    return (*range(far, blocks), *reversed(range(far)))


def solution(mesh):
    placed = (
        P(("groups", "tm"), "head"),
        P("segment", ("groups", "tm"), "head"),
        P("segment", ("groups", "tm"), "head"),
        P("segment", None),
        P("segment", None),
        P("segment", "head"),
        P("groups"),
    )
    blocks = mesh.shape["tm"]
    two_by_two = mesh.shape["segment"] == 2 and mesh.shape["head"] == 2
    mapped = functools.partial(
        jax.shard_map,
        mesh=mesh,
        in_specs=placed,
        out_specs=P("segment", ("groups", "tm"), "head"),
        check_vma=False,
    )

    def run(hidden_in, *rest):
        rows = hidden_in.shape[0] // (mesh.shape["groups"] * blocks)
        features = hidden_in.shape[1] // mesh.shape["head"]
        fits = features % (blocks * HEAD_DIM) == 0 and rows % 32 == 0
        if two_by_two and blocks & (blocks - 1) == 0 and fits:
            step = mapped(by_heads)
        else:
            step = mapped(body)
        return step(hidden_in, *rest)

    return run
```

```python
import functools
import math

import jax
import jax.numpy as jnp
from jax import lax
from jax.experimental import pallas as pl
from jax.experimental.pallas import tpu as pltpu
from jax.sharding import PartitionSpec as P


HEAD_DIM = 128
PART_ROWS = 16
BLOCKED = -1e30


def passed_along(shard, axis, by):
    devices = lax.axis_size(axis)
    pairs = [(i, i + by) for i in range(devices) if 0 <= i + by < devices]
    return lax.ppermute(shard, axis, pairs)


def head_normalize(features, gain_row):
    row_count = features.shape[0]
    shaped = features.astype(jnp.float32).reshape(row_count, -1, HEAD_DIM)
    inverse_rms = lax.rsqrt(jnp.mean(shaped * shaped, axis=-1, keepdims=True) + 1e-06)
    return (shaped * inverse_rms * gain_row).reshape(features.shape).astype(jnp.bfloat16)


def attend_heads(queries, key_rows, value_rows, query_ids, key_ids):
    row_count = queries.shape[0]
    key_count = key_rows.shape[0]
    pair_width = 2 * HEAD_DIM
    group_count = queries.shape[1] // pair_width
    score_scale = 2.0 / math.sqrt(HEAD_DIM)
    allowed = (key_ids[None, :] <= query_ids[:, None]) & (
        key_ids[None, :] >= query_ids[:, None] - 2
    )

    def pair_step(group_index, result):
        column = group_index * pair_width
        query_pair = lax.dynamic_slice_in_dim(queries, column, pair_width, 1).reshape(
            row_count, 2, HEAD_DIM
        )
        key_pair = lax.dynamic_slice_in_dim(key_rows, column, pair_width, 1).reshape(
            key_count, 2, HEAD_DIM
        )
        value_pair = lax.dynamic_slice_in_dim(value_rows, column, pair_width, 1).reshape(
            key_count, 2, HEAD_DIM
        )
        scores = (
            jnp.einsum("rhd,khd->hrk", query_pair, key_pair, preferred_element_type=jnp.float32)
            * score_scale
        )
        weights = jnp.where(allowed[None], jnp.exp(scores), 0.0)
        denominator = jnp.sum(weights, axis=-1)
        mixture = jnp.einsum(
            "hrk,khd->rhd",
            weights.astype(jnp.bfloat16),
            value_pair,
            preferred_element_type=jnp.float32,
        )
        mixture = mixture / jnp.transpose(denominator)[:, :, None]
        return lax.dynamic_update_slice_in_dim(
            result, mixture.reshape(row_count, pair_width), column, 1
        )

    initial = jnp.zeros((row_count, queries.shape[1]), jnp.float32)
    return lax.fori_loop(0, group_count, pair_step, initial)


def body(hidden_in, key_cache, value_cache, query_gain, key_gain, out_gate, span_ids):
    block_rows = hidden_in.shape[0]
    tm_index = lax.axis_index("tm")
    segment_index = lax.axis_index("segment")
    normed_keys = head_normalize(key_cache[0], key_gain[0])
    own_values = value_cache[0]
    first_row = tm_index * block_rows
    all_keys, all_values = (
        lax.all_gather(normed_keys, "tm", axis=0, tiled=True),
        lax.all_gather(own_values, "tm", axis=0, tiled=True),
    )

    def update(row_block):
        queries = head_normalize(row_block, query_gain[0])
        query_ids = lax.dynamic_slice_in_dim(span_ids, first_row, row_block.shape[0], 0)
        mixture = attend_heads(queries, all_keys, all_values, query_ids, span_ids)
        return (row_block.astype(jnp.float32) + out_gate[0] * mixture).astype(jnp.bfloat16)

    segments = lax.axis_size("segment")
    current = hidden_in
    result = hidden_in
    for section in range(segments):
        active = segment_index == section
        produced = lax.cond(active, lambda inputs: update(inputs), lambda inputs: inputs, current)
        result = jnp.where(active, produced, result)
        if section + 1 < segments:
            arrived = passed_along(produced, "segment", 1)
            current = jnp.where(segment_index == section + 1, arrived, current)
    return result[None]


MESH_TAIL = ("tm", "segment", "head")


def swapped(array, offset, blocks, own=True):
    at = lambda t, s, c: (t * 2 + s) * 2 + c
    pairs = [
        (at(t, s, c), at(t ^ offset, c, s))
        for t in range(blocks)
        for s in range(2)
        for c in range(2)
        if own or offset or s != c
    ]
    return lax.ppermute(array, MESH_TAIL, pairs)


def normed(rows, gain):
    rows = rows.astype(jnp.float32)
    inverse_rms = lax.rsqrt(jnp.mean(rows * rows, axis=-1, keepdims=True) + 1e-06)
    return (rows * inverse_rms * gain).astype(jnp.bfloat16)


def split_parts(row):
    high = row.astype(jnp.bfloat16)
    rest = row - high.astype(jnp.float32)
    middle = rest.astype(jnp.bfloat16)
    low = (rest - middle.astype(jnp.float32)).astype(jnp.bfloat16)
    return [part.astype(jnp.float32) for part in (high, middle, low)]


def pack_kernel(pieces, width, key_hbm, value_hbm, hidden_hbm, qgain_hbm, kgain_hbm, gate_hbm, *refs):
    outs, (kgain, qgain, gate, sems) = refs[: len(pieces)], refs[len(pieces) :]
    rows = key_hbm.shape[0]
    half = rows // 2
    tm = lax.axis_index("tm")
    first = pl.multiple_of(lax.axis_index("segment") * half, 16)
    taken = 0

    def start(source, target):
        nonlocal taken
        copy = pltpu.make_async_copy(source, target, sems.at[taken])
        taken += 1
        copy.start()
        return copy

    copies = []
    for out, (offset, head) in zip(outs, pieces):
        base = (tm ^ offset) * width + head * HEAD_DIM
        columns = pl.ds(pl.multiple_of(base, 128), out.shape[1])
        row = [start(key_hbm.at[:, columns], out.at[pl.ds(0, rows)])]
        if not copies:
            row.append(start(kgain_hbm, kgain))
        row += [
            start(value_hbm.at[:, columns], out.at[pl.ds(rows, rows)]),
            start(hidden_hbm.at[pl.ds(first, half), columns], out.at[pl.ds(2 * rows, half)]),
        ]
        if offset == 0:
            row += [start(qgain_hbm, qgain), start(gate_hbm.at[:, columns], gate)]
        copies.append(row)
    for at, (out, (offset, _)) in enumerate(zip(outs, pieces)):
        copies[at][0].wait()
        if at == 0:
            copies[at].pop(1).wait()
        gain = kgain[...]
        for head in range(out.shape[1] // HEAD_DIM):
            lanes = pl.ds(head * HEAD_DIM, HEAD_DIM)
            out[pl.ds(0, rows), lanes] = normed(out[pl.ds(0, rows), lanes], gain)
        for copy in copies[at][1:]:
            copy.wait()
        if offset == 0:
            query_row = jnp.concatenate([qgain[...]] * (width // HEAD_DIM), axis=1)
            parts = split_parts(gate[...]) + split_parts(query_row)
            index = lax.broadcasted_iota(jnp.int32, (PART_ROWS, width), 0)
            table = jnp.zeros((PART_ROWS, width), jnp.float32)
            for line, part in enumerate(parts):
                table = jnp.where(index == line, part, table)
            out[pl.ds(2 * rows + half, PART_ROWS), :] = table.astype(jnp.bfloat16)


def mask_kernel(key_ids, query_ids, bias):
    keys_row, queries_column = key_ids[...], query_ids[...]
    allowed = (keys_row <= queries_column) & (keys_row >= queries_column - 2)
    bias[...] = jnp.where(allowed, 0.0, BLOCKED)


def layer_rows(current, keys, values, bias, query_gain, gate):
    scale = 2.0 / math.sqrt(HEAD_DIM) * math.log2(math.e)
    queries = normed(current, query_gain)
    scores = lax.dot_general(
        queries, keys, (((1,), (1,)), ((), ())), preferred_element_type=jnp.float32
    )
    weights = jnp.exp2(scores * scale + bias)
    denominator = jnp.sum(weights, axis=-1, keepdims=True)
    mixture = jnp.dot(weights.astype(jnp.bfloat16), values, preferred_element_type=jnp.float32)
    mixture = mixture / denominator
    return (current.astype(jnp.float32) + gate * mixture).astype(jnp.bfloat16)


def attend_kernel(offsets, rows, heads, bases, *refs):
    count = len(offsets)
    bias_ref, own, other, outs = refs[0], refs[1 : 1 + count], refs[1 + count : 1 + 2 * count], refs[-count:]
    half = rows // 2

    def run(first, second, last):
        def lanes(at, head):
            return pl.ds((head - bases[at]) * HEAD_DIM, HEAD_DIM)

        def part(source, start, head):
            return jnp.concatenate(
                [ref[pl.ds(start, rows), lanes(at, head)] for at, ref in enumerate(source)], axis=0
            )

        def table(source, line, head):
            at = offsets.index(0)
            block = source[at][pl.ds(2 * rows + half, PART_ROWS), lanes(at, head)]
            block = block.astype(jnp.float32)
            return block[line : line + 1] + (
                block[line + 1 : line + 2] + block[line + 2 : line + 3]
            )

        current = {
            head: jnp.concatenate(
                [
                    ref[pl.ds(2 * rows, half), lanes(at, head)]
                    for at in range(count)
                    for ref in (first[at], second[at])
                ],
                axis=0,
            )
            for head in heads
        }
        bias = bias_ref[...]
        for section in range(last + 1):
            source = (first, second)[section]
            for head in heads:
                current[head] = layer_rows(
                    current[head],
                    part(source, 0, head),
                    part(source, rows, head),
                    bias,
                    table(source, 3, head),
                    table(source, 0, head),
                )
        for head in heads:
            columns = pl.ds(head * HEAD_DIM, HEAD_DIM)
            for at in range(count):
                outs[at][:, columns] = current[head][at * rows : (at + 1) * rows]

    core = lax.axis_index("head")

    @pl.when(core == 0)
    def _():
        run(own, other, 0)

    @pl.when(core != 0)
    def _():
        run(other, own, 1)


def join_kernel(offsets, kept, *refs):
    blocks, out, sems = refs[:-2], refs[-2], refs[-1]
    width = blocks[0].shape[1]
    tm = lax.axis_index("tm")
    stayed = lax.axis_index("segment") == lax.axis_index("head")
    copies = []
    for at, offset in enumerate(offsets):
        target = out.at[:, pl.ds(pl.multiple_of((tm ^ offset) * width, 128), width)]
        copy = pltpu.make_async_copy(blocks[at], target, sems.at[at])
        copies.append(copy)
        if offset == 0:
            mine = pltpu.make_async_copy(kept, target, sems.at[at])

            @pl.when(stayed)
            def _():
                mine.start()

            @pl.when(jnp.logical_not(stayed))
            def _():
                copy.start()

        else:
            copy.start()
    for copy in copies:
        copy.wait()


def grant(size):
    return pltpu.CompilerParams(vmem_limit_bytes=size)


def by_heads(hidden_in, key_cache, value_cache, query_gain, key_gain, out_gate, span_ids):
    rows, features = hidden_in.shape
    blocks = lax.axis_size("tm")
    width = features // blocks
    half = rows // 2
    total = rows * blocks
    tm = lax.axis_index("tm")
    vmem = pl.BlockSpec(memory_space=pltpu.VMEM)
    hbm = pl.BlockSpec(memory_space=pltpu.HBM)
    anywhere = pl.BlockSpec(memory_space=pl.ANY)

    count = width // HEAD_DIM
    groups = [(0, count - 1), (count - 1, 1)] if count > 1 else [(0, 1)]
    sends = send_order(blocks, len(groups))
    offsets = tuple(dict.fromkeys(offset for offset, _ in sends))
    late = sends[-1][0]

    sources = [key_cache[0], value_cache[0], hidden_in, query_gain, key_gain, out_gate]
    sources = [pltpu.with_memory_space_constraint(source, pltpu.HBM) for source in sources]

    def pack(chosen):
        shapes = [
            jax.ShapeDtypeStruct(
                (
                    2 * rows + half + (PART_ROWS if offset == 0 else 0),
                    groups[piece][1] * HEAD_DIM if offset == late else width,
                ),
                jnp.bfloat16,
            )
            for offset, piece in chosen
        ]
        heads = [(offset, groups[piece][0] if offset == late else 0) for offset, piece in chosen]
        return pl.pallas_call(
            functools.partial(pack_kernel, tuple(heads), width),
            out_shape=shapes,
            in_specs=[hbm] * len(sources),
            out_specs=[vmem] * len(shapes),
            scratch_shapes=[
                pltpu.VMEM((1, HEAD_DIM), jnp.float32),
                pltpu.VMEM((1, HEAD_DIM), jnp.float32),
                pltpu.VMEM((1, width), jnp.float32),
                pltpu.SemaphoreType.DMA((3 * len(shapes) + 3,)),
            ],
            compiler_params=grant(4 << 20),
        )(*sources)

    payloads = [*pack(sends[:1]), *pack(sends[1:])]
    own, other = {}, {}
    for key, payload in zip(sends, payloads):
        own[key] = swapped(payload, key[0], blocks)
        other[key] = lax.ppermute(own[key], "head", [(0, 1), (1, 0)])

    ids = jnp.concatenate(
        [lax.dynamic_slice_in_dim(span_ids, (tm ^ offset) * rows, rows, 0) for offset in offsets]
    )
    bias = pl.pallas_call(
        mask_kernel,
        out_shape=jax.ShapeDtypeStruct((total, total), jnp.float32),
        in_specs=[vmem, vmem],
        out_specs=vmem,
        compiler_params=grant(4 << 20),
        name="mask",
    )(ids.reshape(1, total), ids.reshape(total, 1))

    results = []
    for group, (start, heads) in enumerate(groups):
        chosen = [(offset, group if offset == late else 0) for offset in offsets]
        bases = tuple(start if offset == late else 0 for offset in offsets)
        operands = [bias, *[own[key] for key in chosen], *[other[key] for key in chosen], *results]
        results = pl.pallas_call(
            functools.partial(
                attend_kernel, offsets, rows, tuple(range(start, start + heads)), bases
            ),
            out_shape=[jax.ShapeDtypeStruct((rows, width), jnp.bfloat16)] * blocks,
            in_specs=[vmem] * len(operands),
            out_specs=[vmem] * blocks,
            input_output_aliases={1 + 2 * blocks + at: at for at in range(len(results))},
            compiler_params=grant(8 << 20),
        )(*operands)
    back = {}
    for offset in return_order(blocks):
        result = results[offsets.index(offset)]
        back[offset] = swapped(result, offset, blocks, own=False)
    joined = pl.pallas_call(
        functools.partial(join_kernel, offsets),
        out_shape=jax.ShapeDtypeStruct((rows, features), jnp.bfloat16),
        in_specs=[vmem] * (1 + blocks),
        out_specs=anywhere,
        scratch_shapes=[pltpu.SemaphoreType.DMA((blocks,))],
        compiler_params=grant(2 << 20),
        name="join",
    )(results[offsets.index(0)], *[back[offset] for offset in offsets])
    return joined[None]


def send_order(blocks, pieces):
    far = blocks // 2
    late = blocks - 1
    whole = [offset for offset in (far, *range(1, far), *range(far + 1, blocks)) if offset != late]
    split = [(late, piece) for piece in range(pieces)]
    return (*[(offset, 0) for offset in whole], (0, 0), *split)


def return_order(blocks):
    return tuple(reversed(range(blocks)))


def solution(mesh):
    placed = (
        P(("groups", "tm"), "head"),
        P("segment", ("groups", "tm"), "head"),
        P("segment", ("groups", "tm"), "head"),
        P("segment", None),
        P("segment", None),
        P("segment", "head"),
        P("groups"),
    )
    blocks = mesh.shape["tm"]
    two_by_two = mesh.shape["segment"] == 2 and mesh.shape["head"] == 2
    mapped = functools.partial(
        jax.shard_map,
        mesh=mesh,
        in_specs=placed,
        out_specs=P("segment", ("groups", "tm"), "head"),
        check_vma=False,
    )

    def run(hidden_in, *rest):
        rows = hidden_in.shape[0] // (mesh.shape["groups"] * blocks)
        features = hidden_in.shape[1] // mesh.shape["head"]
        fits = features % (blocks * HEAD_DIM) == 0 and rows % 32 == 0
        if two_by_two and blocks & (blocks - 1) == 0 and fits:
            step = mapped(by_heads)
        else:
            step = mapped(body)
        return step(hidden_in, *rest)

    return run
```
